256 devices in a mesh: band: 8 (over y_hi, x), item: 32 (over y_lo, z, core).
Axes of the slice: x: 4, y: 4 (y_hi: 2, y_lo: 2; y = y_hi * 2 + y_lo), z: 8, core: 2. Of those that a mesh axis runs over, the one named last changes fastest.
Arguments:
- ratings: bfloat16 [49152, 16384], P('band', 'item'), may hold values from -6 to 6
- rating_mask: int32 [384, 16384], P('band', 'item'), may hold values 0 or 1
- attributes: bfloat16 [24576, 16384], P('band', 'item'), may hold values from -6 to 6
- attribute_mask: int32 [192, 16384], P('band', 'item'), may hold values 0 or 1
- user_factors: bfloat16 [49152, 256], P('band', 'item'), as said below
- tag_factors: bfloat16 [24576, 256], P('band', 'item'), as said below
Outputs:
- item_factors: float32 [16384, 256], P('item')
The draws below stay inside these ranges and needn't reach their ends.
Inputs may be any that keep to these rules, and one draw needn't show every extreme that they name: `user_factors`: user factors of order one over the square root of 49152. `tag_factors`: tag factors of order one over the square root of 24576.
All inputs are finite; a program needn't handle non-finite values. No bound on the sum of `rating_mask` or of `attribute_mask` on one device may be relied on, other than what follows from the above.
Results may differ from the reference program's by a relative error of at most 0.0003.
Values may be sent and summed in bfloat16 or wider, within the bound.
No kernel may reach another device: no remote copies, remote signals or barrier semaphores. Data moves between devices by JAX's collectives and lax.ppermute only.
A program may use at most 64 MiB of HBM per device.

```python
import jax
import jax.numpy as jnp
from jax import lax

K = 256
BLOCK = 128
I_DEV = 512
USERS = 49152
TAGS = 24576
ITEMS = 16384
N_ITEM = 32


def mixed_factors(key, rows, shift_one, shift_two):
    normal_part = jnp.clip(jax.random.normal(jax.random.fold_in(key, 11), (rows, K), jnp.float32), -4.0, 4.0)
    mixture = normal_part + 0.5 * jnp.roll(normal_part, -shift_one, axis=1) + 0.4 * jnp.roll(normal_part, -shift_two, axis=1)
    scales = jax.random.uniform(jax.random.fold_in(key, 14), (rows, 1), jnp.float32, 0.5, 2.0)
    mixture = mixture * scales / jnp.sqrt(rows * 1.41 * 1.75)
    return mixture


def draw_user_factors(key, part):
    return mixed_factors(jax.random.fold_in(key, 1), USERS, 1, 5).astype(jnp.bfloat16)


def draw_tag_factors(key, part):
    return mixed_factors(jax.random.fold_in(key, 2), TAGS, 2, 7).astype(jnp.bfloat16)


def set_ends(drawn, rng, low, high):
    longest = drawn.shape.index(max(drawn.shape))
    spots = []
    for shift in (0, 1):
        where = [jax.random.randint(jax.random.fold_in(rng, axis), (), 0, length) for axis, length in enumerate(drawn.shape)]
        where[longest] = (where[longest] + shift) % drawn.shape[longest]
        spots.append(tuple(where))
    return drawn.at[spots[0]].set(low).at[spots[1]].set(high)


def level_of(own_key, dims, pieces, least, high):
    loudness = 1.0
    for axis_at, blocks in pieces:
        steps = jax.random.uniform(jax.random.fold_in(jax.random.fold_in(own_key, 6), axis_at), (blocks,), jnp.float32, least / len(pieces), high / len(pieces))
        loudness = loudness * jnp.repeat(jnp.exp(steps), dims[axis_at] // blocks).reshape((-1,) + (1,) * (len(dims) - 1 - axis_at))
    return loudness


def scatter_about(own_key, dims, width, limit, pieces=(), held_as=jnp.bfloat16):
    loudness = level_of(own_key, dims, pieces, -0.22, 0.18) if pieces else 1.0
    result = jax.random.normal(own_key, dims, jnp.float32) * width * loudness
    return jnp.minimum(jnp.maximum(result, -limit), limit).astype(held_as)


def setup_inputs(seed: int = 0) -> dict:
    streams_of = jax.random.split(jax.random.key(seed), 7)
    ratings = scatter_about(streams_of[0], (USERS, ITEMS), 1.0, 6.0, ((0, 8), (1, 32)))
    rating_mask = set_ends((jax.random.randint(streams_of[1], (USERS // BLOCK, ITEMS), 0, 2) < 1).astype(jnp.int32), jax.random.fold_in(streams_of[1], 1), 0, 1)
    attributes = scatter_about(streams_of[2], (TAGS, ITEMS), 1.0, 6.0, ((0, 8), (1, 32)))
    attribute_mask = set_ends((jax.random.randint(streams_of[3], (TAGS // BLOCK, ITEMS), 0, 2) < 1).astype(jnp.int32), jax.random.fold_in(streams_of[3], 1), 0, 1)
    user_factors = draw_user_factors(jax.random.fold_in(streams_of[6], 71), 0)
    tag_factors = draw_tag_factors(jax.random.fold_in(streams_of[6], 71), 0)
    return dict(ratings=ratings, rating_mask=rating_mask, attributes=attributes, attribute_mask=attribute_mask, user_factors=user_factors, tag_factors=tag_factors)


LAMBDA = 0.5
REG = 0.1

def apply_mask(values, mask):
    rows, cols = values.shape
    blocks = mask.shape[0]
    shaped = values.reshape(blocks, rows // blocks, cols) * mask.astype(values.dtype)[:, None, :]
    return shaped.reshape(rows, cols)

def inner(left, right):
    return lax.dot_general(left.astype(jnp.float32), right.astype(jnp.float32), (((0,), (0,)), ((), ())), preferred_element_type=jnp.float32)

def solve_rows(factor, rhs):
    half = lax.linalg.triangular_solve(factor, rhs, left_side=False, lower=True, transpose_a=True)
    return lax.linalg.triangular_solve(factor, half, left_side=False, lower=True, transpose_a=False)

def reference(ratings, rating_mask, attributes, attribute_mask, user_factors, tag_factors):
    gram = inner(user_factors, user_factors) + LAMBDA * inner(tag_factors, tag_factors)
    gram = gram + REG * jnp.eye(K, dtype=jnp.float32)
    factor = jnp.linalg.cholesky(gram)

    def one_block(index):
        start = (index * I_DEV).astype(jnp.int32)
        rate_part = lax.dynamic_slice_in_dim(ratings, start, I_DEV, 1)
        rate_mask = lax.dynamic_slice_in_dim(rating_mask, start, I_DEV, 1)
        attr_part = lax.dynamic_slice_in_dim(attributes, start, I_DEV, 1)
        attr_mask = lax.dynamic_slice_in_dim(attribute_mask, start, I_DEV, 1)
        rhs = inner(apply_mask(rate_part, rate_mask), user_factors)
        rhs = rhs + LAMBDA * inner(apply_mask(attr_part, attr_mask), tag_factors)
        return solve_rows(factor, rhs)
    solved = lax.map(one_block, jnp.arange(N_ITEM, dtype=jnp.int32))
    return solved.reshape(ITEMS, K)
```

```python
import functools

import jax
import jax.numpy as jnp
from jax import lax
from jax.experimental import pallas as pl
from jax.experimental.pallas import tpu as pltpu
from jax.sharding import PartitionSpec as P

LAMBDA = 0.5
REG = 0.1
STEP = 1024
PANEL = 8

NY, NZ, NC = 2, 8, 2
NYH, NX = 2, 4
NT = (((1,), (1,)), ((), ()))


def item_of(y, z, c):
    return ((y % NY) * NZ + z % NZ) * NC + c % NC


def item_perm(dy, dz, dc):
    places = [(y, z, c) for y in range(NY) for z in range(NZ) for c in range(NC)]
    return [(item_of(y, z, c), item_of(y + dy, z + dz, c + dc)) for y, z, c in places]


def band_perm(stage):
    pairs = []
    for yh in range(NYH):
        for x in range(NX):
            for item in range(NY * NZ * NC):
                if stage == 2:
                    to = (1 - yh) * NX + x
                elif stage == item % NC:
                    to = yh * NX + (x ^ 1)
                else:
                    to = yh * NX + (NX - 1 - x)
                pairs.append(((yh * NX + x) * 32 + item, to * 32 + item))
    return pairs


UP = item_perm(0, 1, 0)
DOWN = item_perm(0, -1, 0)
ACROSS = item_perm(1, 0, 0)
CORE = item_perm(0, 0, 1)
OFFSETS = (0, -1, 1, -2, 2, -3, 3, 4)


def gather_columns(own):
    half = own.shape[1] // 2
    up = down = own
    near = [own]
    far = [lax.ppermute(own, "item", ACROSS)]
    for step in range(1, 4):
        up = lax.ppermute(up, "item", UP)
        down = lax.ppermute(down, "item", DOWN)
        both = jnp.concatenate([up, down], axis=0)
        near.append(both)
        far.append(lax.ppermute(both, "item", ACROSS))
    last = jnp.concatenate(
        [lax.ppermute(up[:, :half], "item", UP), lax.ppermute(down[:, half:], "item", DOWN)], axis=1
    )
    near.append(last)
    far.append(lax.ppermute(last, "item", ACROSS))
    return jnp.concatenate(near + far, axis=0)


def gram_kernel(users, mine_ref, other_ref, out_ref):
    step = pl.program_id(0)

    @pl.when(step == 0)
    def _():
        out_ref[...] = jnp.zeros_like(out_ref)

    scale = jnp.where(step < users, 1.0, LAMBDA).astype(jnp.bfloat16)
    mine = mine_ref[...]
    scaled = mine * scale
    out_ref[:, :128] += lax.dot_general(scaled, mine, NT, preferred_element_type=jnp.float32)
    out_ref[:, 128:] += lax.dot_general(scaled, other_ref[...], NT, preferred_element_type=jnp.float32)


def top_gram(mine, other, n_users):
    rows = mine.shape[1]
    spec = pl.BlockSpec((128, STEP), lambda i: (0, i))
    return pl.pallas_call(
        functools.partial(gram_kernel, n_users // STEP),
        out_shape=jax.ShapeDtypeStruct((128, 256), jnp.float32),
        grid=(rows // STEP,),
        in_specs=[spec, spec],
        out_specs=pl.BlockSpec((128, 256), lambda i: (0, 0)),
        name="top_gram",
    )(mine, other)


def rhs_kernel(users, mine_ref, other_ref, rate_ref, rate_mask_ref, attr_ref, attr_mask_ref, out_ref):
    step = pl.program_id(0)

    @pl.when(step == 0)
    def _():
        out_ref[...] = jnp.zeros_like(out_ref)

    def add(value_ref, mask_ref, scale):
        parts = []
        for block in range(STEP // 128):
            keep = mask_ref[0, block : block + 1, :].astype(jnp.float32) * scale
            parts.append(value_ref[block * 128 : (block + 1) * 128, :] * keep.astype(jnp.bfloat16))
        masked = jnp.concatenate(parts, axis=0)
        out_ref[:128, :] += jnp.dot(mine_ref[...], masked, preferred_element_type=jnp.float32)
        out_ref[128:, :] += jnp.dot(other_ref[...], masked, preferred_element_type=jnp.float32)

    @pl.when(step < users)
    def _():
        add(rate_ref, rate_mask_ref, 1.0)

    @pl.when(step >= users)
    def _():
        add(attr_ref, attr_mask_ref, LAMBDA)


def rhs_rows(mine, other, ratings, rating_mask, attributes, attribute_mask):
    users = ratings.shape[0] // STEP
    tags = attributes.shape[0] // STEP
    items = ratings.shape[1]
    blocks = STEP // 128
    factor = pl.BlockSpec((128, STEP), lambda i: (0, i))
    first = lambda i: jnp.minimum(i, users - 1)
    second = lambda i: jnp.maximum(i - users, 0)
    return pl.pallas_call(
        functools.partial(rhs_kernel, users),
        out_shape=jax.ShapeDtypeStruct((256, items), jnp.float32),
        grid=(users + tags,),
        in_specs=[
            factor,
            factor,
            pl.BlockSpec((STEP, items), lambda i: (first(i), 0)),
            pl.BlockSpec((1, blocks, items), lambda i: (first(i), 0, 0)),
            pl.BlockSpec((STEP, items), lambda i: (second(i), 0)),
            pl.BlockSpec((1, blocks, items), lambda i: (second(i), 0, 0)),
        ],
        out_specs=pl.BlockSpec((256, items), lambda i: (0, 0)),
        compiler_params=pltpu.CompilerParams(vmem_limit_bytes=48 << 20),
        name="rhs_rows",
    )(
        mine,
        other,
        ratings,
        rating_mask.reshape(users, blocks, items),
        attributes,
        attribute_mask.reshape(tags, blocks, items),
    )


def inverse_kernel(order_ref, top_ref, peer_ref, out_ref, a_ref):
    n = a_ref.shape[0]
    h = n // 2
    a_ref[:h, :] = top_ref[...]
    a_ref[h:, :h] = peer_ref[:, h:]
    a_ref[h:, h:] = peer_ref[:, :h]
    rows = lax.broadcasted_iota(jnp.int32, (n, n), 0)
    cols = lax.broadcasted_iota(jnp.int32, (n, n), 1)
    a_ref[...] = a_ref[...] + jnp.where(rows == cols, REG, 0.0)
    sub = lax.broadcasted_iota(jnp.int32, (PANEL, n), 0)
    lane = lax.broadcasted_iota(jnp.int32, (PANEL, n), 1)

    for p in range(n // PANEL):
        r0 = p * PANEL
        panel = a_ref[r0 : r0 + PANEL, :]
        before = panel
        for j in range(PANEL):
            k = r0 + j
            column = panel[:, k : k + 1]
            inv = 1.0 / panel[j : j + 1, k : k + 1]
            row = jnp.where(lane[:1] == k, inv, panel[j : j + 1, :] * inv)
            rest = jnp.where(lane == k, 0.0, panel) - column * row
            panel = jnp.where(sub == j, row, rest)
        inside = (rows >= r0) & (rows < r0 + PANEL)
        here = (cols >= r0) & (cols < r0 + PANEL)
        left = a_ref[:, r0 : r0 + PANEL]
        change = jnp.dot(left, panel, preferred_element_type=jnp.float32, precision=lax.Precision.HIGHEST)
        a = jnp.where(here, 0.0, a_ref[...]) - change
        a_ref[...] = a
        a_ref[r0 : r0 + PANEL, :] = panel

    for b in range(n // 8):
        out_ref[pl.ds(pl.multiple_of(order_ref[b] * 8, 8), 8), :] = a_ref[b * 8 : (b + 1) * 8, :]


def ordered_inverse(order, top, peer):
    n = top.shape[1]
    return pl.pallas_call(
        inverse_kernel,
        out_shape=jax.ShapeDtypeStruct((n, n), jnp.float32),
        grid_spec=pltpu.PrefetchScalarGridSpec(
            num_scalar_prefetch=1,
            grid=(1,),
            in_specs=[pl.BlockSpec(top.shape, lambda i, o: (0, 0)), pl.BlockSpec(top.shape, lambda i, o: (0, 0))],
            out_specs=pl.BlockSpec((n, n), lambda i, o: (0, 0)),
            scratch_shapes=[pltpu.VMEM((n, n), jnp.float32)],
        ),
        name="ordered_inverse",
    )(order, top, peer)


def final_kernel(rhs_ref, more_ref, inverse_ref, out_ref):
    rhs = rhs_ref[...] + more_ref[...]
    out_ref[...] = lax.dot_general(
        rhs,
        inverse_ref[...],
        (((0,), (1,)), ((), ())),
        preferred_element_type=jnp.float32,
        precision=lax.Precision.HIGHEST,
    )


def final_solve(rhs, more, inverse):
    k, items = rhs.shape
    return pl.pallas_call(
        final_kernel,
        out_shape=jax.ShapeDtypeStruct((items, k), jnp.float32),
        name="final_solve",
    )(rhs, more, inverse)


def both(value, stage):
    return value + lax.ppermute(value, ("band", "item"), band_perm(stage))


def body(ratings, rating_mask, attributes, attribute_mask, user_factors, tag_factors):
    n_users = user_factors.shape[0]
    own = jnp.concatenate([user_factors.T, tag_factors.T], axis=1)
    mine = gather_columns(own)
    other = lax.ppermute(mine, "item", CORE)

    item = lax.axis_index("item")
    y, z, c = item // (NZ * NC), (item // NC) % NZ, item % NC
    order = []
    for dc in range(2):
        for dy in range(2):
            for dz in OFFSETS:
                order.append((((y + dy) % NY) * NZ + (z + dz) % NZ) * NC + (c + dc) % NC)
    order = jnp.stack(order).astype(jnp.int32)

    top = top_gram(mine, other, n_users)
    rhs = rhs_rows(mine, other, ratings, rating_mask, attributes, attribute_mask)
    for stage in range(3):
        top = both(top, stage)
    peer = lax.ppermute(top, "item", CORE)
    inverse = ordered_inverse(order, top, peer)
    for stage in range(2):
        rhs = both(rhs, stage)
    more = lax.ppermute(rhs, ("band", "item"), band_perm(2))
    return final_solve(rhs, more, inverse)


def solution(mesh):
    spec = P("band", "item")
    return jax.shard_map(
        body, mesh=mesh, in_specs=(spec,) * 6, out_specs=P("item", None), check_vma=False
    )
```

```python
import functools

import jax
import jax.numpy as jnp
from jax import lax
from jax.experimental import pallas as pl
from jax.experimental.pallas import tpu as pltpu
from jax.sharding import PartitionSpec as P

LAMBDA = 0.5
REG = 0.1
SUB = 8
BLOCK = 32

NY, NZ, NC = 2, 8, 2
NYH, NX = 2, 4
NT = (((1,), (1,)), ((), ()))


def item_of(y, z, c):
    return ((y % NY) * NZ + z % NZ) * NC + c % NC


def item_perm(dy, dz, dc):
    places = [(y, z, c) for y in range(NY) for z in range(NZ) for c in range(NC)]
    return [(item_of(y, z, c), item_of(y + dy, z + dz, c + dc)) for y, z, c in places]


def band_perm(stage):
    pairs = []
    for yh in range(NYH):
        for x in range(NX):
            for item in range(NY * NZ * NC):
                if stage == 2:
                    to = (1 - yh) * NX + x
                elif stage == item % NC:
                    to = yh * NX + (x ^ 1)
                else:
                    to = yh * NX + (NX - 1 - x)
                pairs.append(((yh * NX + x) * 32 + item, to * 32 + item))
    return pairs


UP = item_perm(0, 1, 0)
DOWN = item_perm(0, -1, 0)
ACROSS = item_perm(1, 0, 0)
CORE = item_perm(0, 0, 1)


def gather_columns(own):
    half = own.shape[1] // 2
    up = down = own
    near, far = [own], []
    pending = own
    for step in range(1, 4):
        far.append(lax.ppermute(pending, "item", ACROSS))
        down = lax.ppermute(down, "item", DOWN)
        up = lax.ppermute(up, "item", UP)
        pending = jnp.concatenate([up, down], axis=0)
        near.append(pending)
    far.append(lax.ppermute(pending, "item", ACROSS))
    last = jnp.concatenate(
        [lax.ppermute(up[:, :half], "item", UP), lax.ppermute(down[:, half:], "item", DOWN)], axis=1
    )
    first_part = near + far[:3]
    second_part = [last, far[3], lax.ppermute(last, "item", ACROSS)]
    return jnp.concatenate(first_part, axis=0), jnp.concatenate(second_part, axis=0)


PLACES = [(0, dz) for dz in (0, -1, 1, -2, 2, -3, 3)] + [(1, dz) for dz in (0, -1, 1, -2, 2)]
PLACES += [(0, 4), (1, -3), (1, 3), (1, 4)]


def whole():
    return pl.BlockSpec(memory_space=pltpu.VMEM)


def mask_kernel(scale, value_ref, mask_ref, out_ref):
    for block in range(mask_ref.shape[0]):
        rows = slice(block * 128, (block + 1) * 128)
        keep = (mask_ref[block : block + 1, :].astype(jnp.float32) * scale).astype(jnp.bfloat16)
        out_ref[rows, :] = value_ref[rows, :] * keep


def masked(values, mask, scale, name):
    return pl.pallas_call(
        functools.partial(mask_kernel, scale),
        out_shape=jax.ShapeDtypeStruct(values.shape, values.dtype),
        in_specs=[whole(), whole()],
        out_specs=whole(),
        compiler_params=pltpu.CompilerParams(vmem_limit_bytes=4 << 20),
        name=name,
    )(values, mask)


def weighted_gram(left_ref, right_ref, users):
    total = lax.dot_general(left_ref[:, :users], right_ref[:, :users], NT, preferred_element_type=jnp.float32)
    tags = lax.dot_general(left_ref[:, users:], right_ref[:, users:], NT, preferred_element_type=jnp.float32)
    return total + LAMBDA * tags


def gram_kernel(users, mine_ref, other_ref, out_ref):
    out_ref[:, :128] = weighted_gram(mine_ref, mine_ref, users)
    out_ref[:, 128:] = weighted_gram(mine_ref, other_ref, users)


def top_gram(mine, other, n_users):
    return pl.pallas_call(
        functools.partial(gram_kernel, n_users),
        out_shape=jax.ShapeDtypeStruct((128, 256), jnp.float32),
        in_specs=[whole(), whole()],
        out_specs=whole(),
        compiler_params=pltpu.CompilerParams(vmem_limit_bytes=4 << 20),
        name="top_gram",
    )(mine, other)


def rhs_kernel(factor_ref, *refs):
    parts, out_ref = refs[:-1], refs[-1]
    start = 0
    total = None
    for part_ref in parts:
        rows = part_ref.shape[0]
        product = jnp.dot(factor_ref[:, start : start + rows], part_ref[...], preferred_element_type=jnp.float32)
        total = product if total is None else total + product
        start += rows
    out_ref[...] = total


def rhs_rows(factor, parts, name):
    return pl.pallas_call(
        rhs_kernel,
        out_shape=jax.ShapeDtypeStruct((factor.shape[0], parts[0].shape[1]), jnp.float32),
        in_specs=[whole()] * (1 + len(parts)),
        out_specs=whole(),
        compiler_params=pltpu.CompilerParams(vmem_limit_bytes=4 << 20),
        name=name,
    )(factor, *parts)


def spread(x):
    return jnp.broadcast_to(x, (SUB, 128))


def small_inverse(columns, sub):
    for j in range(SUB):
        hit = sub == j
        pivot = columns[j]
        inv = 1.0 / spread(pivot[j : j + 1, :])
        new = []
        for m in range(SUB):
            if m == j:
                new.append(jnp.where(hit, inv, -pivot * inv))
            else:
                row = spread(columns[m][j : j + 1, :]) * inv
                new.append(jnp.where(hit, row, columns[m] - pivot * row))
        columns = new
    return columns


def weighted_rows(weights, rows):
    total = weights[0] * rows[0]
    for weight, row in zip(weights[1:], rows[1:]):
        total = total + weight * row
    return total


def inverse_kernel(order_ref, top_ref, peer_ref, out_ref, a_ref):
    n = a_ref.shape[0]
    h = n // 2
    a_ref[:h, :] = top_ref[...]
    a_ref[h:, :h] = peer_ref[:, h:]
    a_ref[h:, h:] = peer_ref[:, :h]
    sub = lax.broadcasted_iota(jnp.int32, (SUB, 128), 0)
    lane = lax.broadcasted_iota(jnp.int32, (SUB, 128), 1)
    wide = lax.broadcasted_iota(jnp.int32, (1, 128), 1)
    for r in range(0, n, SUB):
        at = slice(r // 128 * 128, r // 128 * 128 + 128)
        a_ref[r : r + SUB, at] += jnp.where(lane == sub + r % 128, REG, 0.0)

    panels = BLOCK // SUB
    ahead = None
    for r0 in range(0, n, BLOCK):
        side = r0 // 128
        base = r0 % 128
        panel = []
        for q in range(panels):
            rows = slice(r0 + q * SUB, r0 + (q + 1) * SUB)
            panel.append([a_ref[rows, :128], a_ref[rows, 128:]])
        if ahead is not None:
            panel[0] = ahead
        for q in range(panels):
            k = base + q * SUB
            inside = (lane >= k) & (lane < k + SUB)
            small = small_inverse([spread(panel[q][side][:, k + m : k + m + 1]) for m in range(SUB)], sub)
            fresh = []
            for s in range(2):
                value = weighted_rows(small, [spread(panel[q][s][m : m + 1, :]) for m in range(SUB)])
                if s == side:
                    for m in range(SUB):
                        value = jnp.where(lane == k + m, small[m], value)
                fresh.append(value)
            panel[q] = fresh
            rows = [[spread(fresh[s][m : m + 1, :]) for m in range(SUB)] for s in range(2)]
            for i in range(panels):
                if i == q:
                    continue
                left = [spread(panel[i][side][:, k + m : k + m + 1]) for m in range(SUB)]
                for s in range(2):
                    old = panel[i][s]
                    if s == side:
                        old = jnp.where(inside, 0.0, old)
                    panel[i][s] = old - weighted_rows(left, rows[s])
        block = jnp.concatenate([jnp.concatenate(panel[q], axis=1) for q in range(panels)], axis=0)
        r1 = r0 + BLOCK
        if r1 < n:
            left = [spread(a_ref[r1 : r1 + SUB, r0 + m : r0 + m + 1]) for m in range(BLOCK)]
            ahead = []
            for s in range(2):
                old = a_ref[r1 : r1 + SUB, s * 128 : (s + 1) * 128]
                if s == side:
                    old = jnp.where((lane >= base) & (lane < base + BLOCK), 0.0, old)
                for q in range(panels):
                    rows = [spread(panel[q][s][m : m + 1, :]) for m in range(SUB)]
                    old = old - weighted_rows(left[q * SUB : (q + 1) * SUB], rows)
                ahead.append(old)
        change = jnp.dot(a_ref[:, r0:r1], block, preferred_element_type=jnp.float32, precision=lax.Precision.HIGHEST)
        for s in range(2):
            at = slice(s * 128, (s + 1) * 128)
            old = a_ref[:, at]
            if s == side:
                old = jnp.where((wide >= base) & (wide < base + BLOCK), 0.0, old)
            a_ref[:, at] = old - change[:, at]
        a_ref[r0:r1, :] = block

    for b in range(n // 8):
        out_ref[pl.ds(pl.multiple_of(order_ref[b] * 8, 8), 8), :] = a_ref[b * 8 : (b + 1) * 8, :]


def ordered_inverse(order, top, peer):
    n = top.shape[1]
    return pl.pallas_call(
        inverse_kernel,
        out_shape=jax.ShapeDtypeStruct((n, n), jnp.float32),
        in_specs=[pl.BlockSpec(memory_space=pltpu.SMEM), whole(), whole()],
        out_specs=whole(),
        scratch_shapes=[pltpu.VMEM((n, n), jnp.float32)],
        compiler_params=pltpu.CompilerParams(vmem_limit_bytes=4 << 20),
        cost_estimate=pl.CostEstimate(flops=3 * 10**10, bytes_accessed=10**8, transcendentals=0),
        name="ordered_inverse",
    )(order, top, peer)


def final_kernel(rhs_ref, more_ref, inverse_ref, out_ref):
    out_ref[...] = lax.dot_general(
        rhs_ref[...] + more_ref[...],
        inverse_ref[...],
        (((0,), (1,)), ((), ())),
        preferred_element_type=jnp.float32,
        precision=lax.Precision.HIGHEST,
    )


def final_solve(*values):
    k, items = values[0].shape
    return pl.pallas_call(
        final_kernel,
        out_shape=jax.ShapeDtypeStruct((items, k), jnp.float32),
        in_specs=[whole()] * len(values),
        out_specs=whole(),
        compiler_params=pltpu.CompilerParams(vmem_limit_bytes=8 << 20),
        name="final_solve",
    )(*values)


def swap(value, stage):
    return lax.ppermute(value, ("band", "item"), band_perm(stage))


def body(ratings, rating_mask, attributes, attribute_mask, user_factors, tag_factors):
    n_users = user_factors.shape[0]
    own = jnp.concatenate([user_factors.T, tag_factors.T], axis=1)
    first, second = gather_columns(own)
    other_first = lax.ppermute(first, "item", CORE)
    other_second = lax.ppermute(second, "item", CORE)
    mine = jnp.concatenate([first, second], axis=0)
    other = jnp.concatenate([other_first, other_second], axis=0)

    parts = [
        masked(ratings, rating_mask, 1.0, "mask_users"),
        masked(attributes, attribute_mask, LAMBDA, "mask_tags"),
    ]

    item = lax.axis_index("item")
    y, z, c = item // (NZ * NC), (item // NC) % NZ, item % NC
    dc = jnp.repeat(jnp.arange(2, dtype=jnp.int32), 16)
    dy = jnp.array([p[0] for p in PLACES] * 2, jnp.int32)
    dz = jnp.array([p[1] + NZ for p in PLACES] * 2, jnp.int32)
    order = (((y + dy) % NY) * NZ + (z + dz) % NZ) * NC + (c + dc) % NC

    rhs_mine = rhs_rows(mine, parts, "rhs_mine")
    top = top_gram(mine, other, n_users)
    top, later = lax.optimization_barrier((top, other))
    rhs_other = rhs_rows(later, parts, "rhs_other")

    fresh, peer_mine, rhs_other = lax.optimization_barrier((swap(top, 0), swap(rhs_mine, 0), rhs_other))
    top = top + fresh
    rhs_mine = rhs_mine + peer_mine
    fresh, peer_other = lax.optimization_barrier((swap(top, 1), swap(rhs_other, 0)))
    top = top + fresh
    rhs = jnp.concatenate([rhs_mine, rhs_other + peer_other], axis=0)
    rhs = rhs + swap(rhs, 1)
    top = top + swap(top, 2)
    inverse = ordered_inverse(order, top, lax.ppermute(top, "item", CORE))
    return final_solve(rhs, swap(rhs, 2), inverse)


def solution(mesh):
    spec = P("band", "item")
    return jax.shard_map(
        body, mesh=mesh, in_specs=(spec,) * 6, out_specs=P("item", None), check_vma=False
    )
```

```python
import functools

import jax
import jax.numpy as jnp
from jax import lax
from jax.experimental import pallas as pl
from jax.experimental.pallas import tpu as pltpu
from jax.sharding import PartitionSpec as P

LAMBDA = 0.5
REG = 0.1
SUB = 8
BLOCK = 16

NY, NZ, NC = 2, 8, 2
NYH, NX = 2, 4
NT = (((1,), (1,)), ((), ()))


def item_of(y, z, c):
    return ((y % NY) * NZ + z % NZ) * NC + c % NC


def item_perm(dy, dz, dc):
    places = [(y, z, c) for y in range(NY) for z in range(NZ) for c in range(NC)]
    return [(item_of(y, z, c), item_of(y + dy, z + dz, c + dc)) for y, z, c in places]


def band_perm(stage):
    pairs = []
    for yh in range(NYH):
        for x in range(NX):
            for item in range(NY * NZ * NC):
                if stage == 2:
                    to = (1 - yh) * NX + x
                elif stage == item % NC:
                    to = yh * NX + (x ^ 1)
                else:
                    to = yh * NX + (NX - 1 - x)
                pairs.append(((yh * NX + x) * 32 + item, to * 32 + item))
    return pairs


UP = item_perm(0, 1, 0)
DOWN = item_perm(0, -1, 0)
ACROSS = item_perm(1, 0, 0)
CORE = item_perm(0, 0, 1)


def gather_columns(own):
    half = own.shape[1] // 2
    up = down = own
    near, far = [own], []
    pending = own
    for step in range(1, 4):
        far.append(lax.ppermute(pending, "item", ACROSS))
        down = lax.ppermute(down, "item", DOWN)
        up = lax.ppermute(up, "item", UP)
        pending = jnp.concatenate([up, down], axis=0)
        near.append(pending)
    far.append(lax.ppermute(pending, "item", ACROSS))
    last = jnp.concatenate(
        [lax.ppermute(up[:, :half], "item", UP), lax.ppermute(down[:, half:], "item", DOWN)], axis=1
    )
    first_part = near + far[:3]
    second_part = [last, far[3], lax.ppermute(last, "item", ACROSS)]
    return jnp.concatenate(first_part, axis=0), jnp.concatenate(second_part, axis=0)


PLACES = [(0, dz) for dz in (0, -1, 1, -2, 2, -3, 3)] + [(1, dz) for dz in (0, -1, 1, -2, 2)]
PLACES += [(0, 4), (1, -3), (1, 3), (1, 4)]


def whole():
    return pl.BlockSpec(memory_space=pltpu.VMEM)


def mask_kernel(scale, value_ref, mask_ref, out_ref):
    for block in range(mask_ref.shape[0]):
        rows = slice(block * 128, (block + 1) * 128)
        keep = (mask_ref[block : block + 1, :].astype(jnp.float32) * scale).astype(jnp.bfloat16)
        out_ref[rows, :] = value_ref[rows, :] * keep


def masked(values, mask, scale, name):
    return pl.pallas_call(
        functools.partial(mask_kernel, scale),
        out_shape=jax.ShapeDtypeStruct(values.shape, values.dtype),
        in_specs=[whole(), whole()],
        out_specs=whole(),
        compiler_params=pltpu.CompilerParams(vmem_limit_bytes=4 << 20),
        name=name,
    )(values, mask)


def weighted_gram(left_ref, right_ref, users):
    total = lax.dot_general(left_ref[:, :users], right_ref[:, :users], NT, preferred_element_type=jnp.float32)
    tags = lax.dot_general(left_ref[:, users:], right_ref[:, users:], NT, preferred_element_type=jnp.float32)
    return total + LAMBDA * tags


def gram_kernel(users, mine_ref, other_ref, out_ref):
    out_ref[:, :128] = weighted_gram(mine_ref, mine_ref, users)
    out_ref[:, 128:] = weighted_gram(mine_ref, other_ref, users)


def top_gram(mine, other, n_users):
    return pl.pallas_call(
        functools.partial(gram_kernel, n_users),
        out_shape=jax.ShapeDtypeStruct((128, 256), jnp.float32),
        in_specs=[whole(), whole()],
        out_specs=whole(),
        compiler_params=pltpu.CompilerParams(vmem_limit_bytes=4 << 20),
        name="top_gram",
    )(mine, other)


def rhs_kernel(factor_ref, *refs):
    parts, out_ref = refs[:-1], refs[-1]
    start = 0
    total = None
    for part_ref in parts:
        rows = part_ref.shape[0]
        product = jnp.dot(factor_ref[:, start : start + rows], part_ref[...], preferred_element_type=jnp.float32)
        total = product if total is None else total + product
        start += rows
    out_ref[...] = total


def rhs_rows(factor, parts, name):
    return pl.pallas_call(
        rhs_kernel,
        out_shape=jax.ShapeDtypeStruct((factor.shape[0], parts[0].shape[1]), jnp.float32),
        in_specs=[whole()] * (1 + len(parts)),
        out_specs=whole(),
        compiler_params=pltpu.CompilerParams(vmem_limit_bytes=4 << 20),
        name=name,
    )(factor, *parts)


def spread(x):
    return jnp.broadcast_to(x, (SUB, 128))


def small_inverse(columns, sub):
    for j in range(SUB):
        hit = sub == j
        pivot = columns[j]
        inv = 1.0 / spread(pivot[j : j + 1, :])
        new = []
        for m in range(SUB):
            if m == j:
                new.append(jnp.where(hit, inv, -pivot * inv))
            else:
                row = spread(columns[m][j : j + 1, :]) * inv
                new.append(jnp.where(hit, row, columns[m] - pivot * row))
        columns = new
    return columns


def weighted_rows(weights, rows):
    total = weights[0] * rows[0]
    for weight, row in zip(weights[1:], rows[1:]):
        total = total + weight * row
    return total


def inverse_kernel(order_ref, top_ref, peer_ref, out_ref, a_ref):
    n = a_ref.shape[0]
    h = n // 2
    a_ref[:h, :] = top_ref[...]
    a_ref[h:, :h] = peer_ref[:, h:]
    a_ref[h:, h:] = peer_ref[:, :h]
    sub = lax.broadcasted_iota(jnp.int32, (SUB, 128), 0)
    lane = lax.broadcasted_iota(jnp.int32, (SUB, 128), 1)
    wide = lax.broadcasted_iota(jnp.int32, (1, 128), 1)
    for r in range(0, n, SUB):
        at = slice(r // 128 * 128, r // 128 * 128 + 128)
        a_ref[r : r + SUB, at] += jnp.where(lane == sub + r % 128, REG, 0.0)

    panels = BLOCK // SUB
    ahead = None
    for r0 in range(0, n, BLOCK):
        side = r0 // 128
        base = r0 % 128
        panel = []
        for q in range(panels):
            rows = slice(r0 + q * SUB, r0 + (q + 1) * SUB)
            panel.append([a_ref[rows, :128], a_ref[rows, 128:]])
        if ahead is not None:
            panel[0] = ahead
        for q in range(panels):
            k = base + q * SUB
            inside = (lane >= k) & (lane < k + SUB)
            small = small_inverse([spread(panel[q][side][:, k + m : k + m + 1]) for m in range(SUB)], sub)
            fresh = []
            for s in range(2):
                value = weighted_rows(small, [spread(panel[q][s][m : m + 1, :]) for m in range(SUB)])
                if s == side:
                    for m in range(SUB):
                        value = jnp.where(lane == k + m, small[m], value)
                fresh.append(value)
            panel[q] = fresh
            rows = [[spread(fresh[s][m : m + 1, :]) for m in range(SUB)] for s in range(2)]
            for i in range(panels):
                if i == q:
                    continue
                left = [spread(panel[i][side][:, k + m : k + m + 1]) for m in range(SUB)]
                for s in range(2):
                    old = panel[i][s]
                    if s == side:
                        old = jnp.where(inside, 0.0, old)
                    panel[i][s] = old - weighted_rows(left, rows[s])
        block = jnp.concatenate([jnp.concatenate(panel[q], axis=1) for q in range(panels)], axis=0)
        r1 = r0 + BLOCK
        inside = (wide >= base) & (wide < base + BLOCK)

        def update(low, high):
            change = jnp.dot(
                a_ref[low:high, r0:r1], block, preferred_element_type=jnp.float32, precision=lax.Precision.HIGHEST
            )
            for s in range(2):
                at = slice(s * 128, (s + 1) * 128)
                old = a_ref[low:high, at]
                if s == side:
                    old = jnp.where(inside, 0.0, old)
                a_ref[low:high, at] = old - change[:, at]

        if r1 < n:
            left = [spread(a_ref[r1 : r1 + SUB, r0 + m : r0 + m + 1]) for m in range(BLOCK)]
            ahead = []
            for s in range(2):
                old = a_ref[r1 : r1 + SUB, s * 128 : (s + 1) * 128]
                if s == side:
                    old = jnp.where((lane >= base) & (lane < base + BLOCK), 0.0, old)
                change = None
                for q in range(panels):
                    rows = [spread(panel[q][s][m : m + 1, :]) for m in range(SUB)]
                    part = weighted_rows(left[q * SUB : (q + 1) * SUB], rows)
                    change = part if change is None else change + part
                ahead.append(old - change)
            update(r1, r1 + BLOCK)
            if r1 + BLOCK < n:
                update(r1 + BLOCK, n)
        if r0 > 0:
            update(0, r0)
        a_ref[r0:r1, :] = block

    for b in range(n // 8):
        out_ref[pl.ds(pl.multiple_of(order_ref[b] * 8, 8), 8), :] = a_ref[b * 8 : (b + 1) * 8, :]


def ordered_inverse(order, top, peer):
    n = top.shape[1]
    return pl.pallas_call(
        inverse_kernel,
        out_shape=jax.ShapeDtypeStruct((n, n), jnp.float32),
        in_specs=[pl.BlockSpec(memory_space=pltpu.SMEM), whole(), whole()],
        out_specs=whole(),
        scratch_shapes=[pltpu.VMEM((n, n), jnp.float32)],
        compiler_params=pltpu.CompilerParams(vmem_limit_bytes=4 << 20),
        cost_estimate=pl.CostEstimate(flops=2 * 10**9, bytes_accessed=0, transcendentals=0),
        name="ordered_inverse",
    )(order, top, peer)


def final_kernel(rhs_ref, more_ref, inverse_ref, out_ref):
    out_ref[...] = lax.dot_general(
        rhs_ref[...] + more_ref[...],
        inverse_ref[...],
        (((0,), (1,)), ((), ())),
        preferred_element_type=jnp.float32,
        precision=lax.Precision.HIGHEST,
    )


def final_solve(*values):
    k, items = values[0].shape
    return pl.pallas_call(
        final_kernel,
        out_shape=jax.ShapeDtypeStruct((items, k), jnp.float32),
        in_specs=[whole()] * len(values),
        out_specs=whole(),
        compiler_params=pltpu.CompilerParams(vmem_limit_bytes=8 << 20),
        name="final_solve",
    )(*values)


def swap(value, stage):
    return lax.ppermute(value, ("band", "item"), band_perm(stage))


def body(ratings, rating_mask, attributes, attribute_mask, user_factors, tag_factors):
    n_users = user_factors.shape[0]
    own = jnp.concatenate([user_factors.T, tag_factors.T], axis=1)
    first, second = gather_columns(own)
    other_first = lax.ppermute(first, "item", CORE)
    other_second = lax.ppermute(second, "item", CORE)
    mine = jnp.concatenate([first, second], axis=0)
    other = jnp.concatenate([other_first, other_second], axis=0)

    parts = [
        masked(ratings, rating_mask, 1.0, "mask_users"),
        masked(attributes, attribute_mask, LAMBDA, "mask_tags"),
    ]

    item = lax.axis_index("item")
    y, z, c = item // (NZ * NC), (item // NC) % NZ, item % NC
    dc = jnp.repeat(jnp.arange(2, dtype=jnp.int32), 16)
    dy = jnp.array([p[0] for p in PLACES] * 2, jnp.int32)
    dz = jnp.array([p[1] + NZ for p in PLACES] * 2, jnp.int32)
    order = (((y + dy) % NY) * NZ + (z + dz) % NZ) * NC + (c + dc) % NC

    rhs_mine = rhs_rows(mine, parts, "rhs_mine")
    top = top_gram(mine, other, n_users)
    top, later = lax.optimization_barrier((top, other))
    rhs_other = rhs_rows(later, parts, "rhs_other")

    fresh, peer_mine, peer_other = lax.optimization_barrier((swap(top, 0), swap(rhs_mine, 0), swap(rhs_other, 0)))
    top = top + fresh
    rhs = jnp.concatenate([rhs_mine + peer_mine, rhs_other + peer_other], axis=0)
    top = top + swap(top, 2)
    rhs = rhs + swap(rhs, 1)
    top = top + swap(top, 1)
    inverse = ordered_inverse(order, top, lax.ppermute(top, "item", CORE))
    return final_solve(rhs, swap(rhs, 2), inverse)


def solution(mesh):
    spec = P("band", "item")
    return jax.shard_map(
        body, mesh=mesh, in_specs=(spec,) * 6, out_specs=P("item", None), check_vma=False
    )
```

```python
import functools

import jax
import jax.numpy as jnp
from jax import lax
from jax.experimental import pallas as pl
from jax.experimental.pallas import tpu as pltpu
from jax.sharding import PartitionSpec as P

LAMBDA = 0.5
REG = 0.1
SUB = 8
BLOCK = 16

NY, NZ, NC = 2, 8, 2
NYH, NX = 2, 4
NT = (((1,), (1,)), ((), ()))


def item_of(y, z, c):
    return ((y % NY) * NZ + z % NZ) * NC + c % NC


def item_perm(dy, dz, dc):
    places = [(y, z, c) for y in range(NY) for z in range(NZ) for c in range(NC)]
    return [(item_of(y, z, c), item_of(y + dy, z + dz, c + dc)) for y, z, c in places]


def band_perm(stage):
    pairs = []
    for yh in range(NYH):
        for x in range(NX):
            for item in range(NY * NZ * NC):
                if stage == 2:
                    to = (1 - yh) * NX + x
                elif stage == item % NC:
                    to = yh * NX + (x ^ 1)
                else:
                    to = yh * NX + (NX - 1 - x)
                pairs.append(((yh * NX + x) * 32 + item, to * 32 + item))
    return pairs


UP = item_perm(0, 1, 0)
DOWN = item_perm(0, -1, 0)
ACROSS = item_perm(1, 0, 0)
CORE = item_perm(0, 0, 1)


def gather_columns(own):
    half = own.shape[1] // 2
    up = down = own
    near, far = [own], []
    pending = own
    for step in range(1, 4):
        far.append(lax.ppermute(pending, "item", ACROSS))
        down = lax.ppermute(down, "item", DOWN)
        up = lax.ppermute(up, "item", UP)
        pending = jnp.concatenate([up, down], axis=0)
        near.append(pending)
    far.append(lax.ppermute(pending, "item", ACROSS))
    last = jnp.concatenate(
        [lax.ppermute(up[:, :half], "item", UP), lax.ppermute(down[:, half:], "item", DOWN)], axis=1
    )
    first_part = near + far[:3]
    second_part = [last, far[3], lax.ppermute(last, "item", ACROSS)]
    return jnp.concatenate(first_part, axis=0), jnp.concatenate(second_part, axis=0)


PLACES = [(0, dz) for dz in (0, -1, 1, -2, 2, -3, 3)] + [(1, dz) for dz in (0, -1, 1, -2, 2)]
PLACES += [(0, 4), (1, -3), (1, 3), (1, 4)]


def whole():
    return pl.BlockSpec(memory_space=pltpu.VMEM)


def mask_kernel(scale, value_ref, mask_ref, out_ref):
    for block in range(mask_ref.shape[0]):
        rows = slice(block * 128, (block + 1) * 128)
        keep = (mask_ref[block : block + 1, :].astype(jnp.float32) * scale).astype(jnp.bfloat16)
        out_ref[rows, :] = value_ref[rows, :] * keep


def masked(values, mask, scale, name):
    return pl.pallas_call(
        functools.partial(mask_kernel, scale),
        out_shape=jax.ShapeDtypeStruct(values.shape, values.dtype),
        in_specs=[whole(), whole()],
        out_specs=whole(),
        compiler_params=pltpu.CompilerParams(vmem_limit_bytes=4 << 20),
        name=name,
    )(values, mask)


def weighted_gram(left_ref, right_ref, users):
    total = lax.dot_general(left_ref[:, :users], right_ref[:, :users], NT, preferred_element_type=jnp.float32)
    tags = lax.dot_general(left_ref[:, users:], right_ref[:, users:], NT, preferred_element_type=jnp.float32)
    return total + LAMBDA * tags


def own_kernel(users, mine_ref, out_ref):
    out_ref[...] = weighted_gram(mine_ref, mine_ref, users)


def gram_kernel(users, own_ref, mine_ref, other_ref, out_ref):
    out_ref[:, :128] = own_ref[...]
    out_ref[:, 128:] = weighted_gram(mine_ref, other_ref, users)


def own_gram(mine, n_users):
    return pl.pallas_call(
        functools.partial(own_kernel, n_users),
        out_shape=jax.ShapeDtypeStruct((128, 128), jnp.float32),
        in_specs=[whole()],
        out_specs=whole(),
        compiler_params=pltpu.CompilerParams(vmem_limit_bytes=4 << 20),
        name="own_gram",
    )(mine)


def top_gram(own, mine, other, n_users):
    return pl.pallas_call(
        functools.partial(gram_kernel, n_users),
        out_shape=jax.ShapeDtypeStruct((128, 256), jnp.float32),
        in_specs=[whole()] * 3,
        out_specs=whole(),
        compiler_params=pltpu.CompilerParams(vmem_limit_bytes=4 << 20),
        name="top_gram",
    )(own, mine, other)


def rhs_kernel(factor_ref, *refs):
    parts, out_ref = refs[:-1], refs[-1]
    start = 0
    total = None
    for part_ref in parts:
        rows = part_ref.shape[0]
        product = jnp.dot(factor_ref[:, start : start + rows], part_ref[...], preferred_element_type=jnp.float32)
        total = product if total is None else total + product
        start += rows
    out_ref[...] = total


def rhs_rows(factor, parts, name):
    return pl.pallas_call(
        rhs_kernel,
        out_shape=jax.ShapeDtypeStruct((factor.shape[0], parts[0].shape[1]), jnp.float32),
        in_specs=[whole()] * (1 + len(parts)),
        out_specs=whole(),
        compiler_params=pltpu.CompilerParams(vmem_limit_bytes=4 << 20),
        name=name,
    )(factor, *parts)


def spread(x):
    return jnp.broadcast_to(x, (SUB, 128))


def small_inverse(columns, sub):
    for j in range(SUB):
        hit = sub == j
        pivot = columns[j]
        inv = 1.0 / spread(pivot[j : j + 1, :])
        new = []
        for m in range(SUB):
            if m == j:
                new.append(jnp.where(hit, inv, -pivot * inv))
            else:
                row = spread(columns[m][j : j + 1, :]) * inv
                new.append(jnp.where(hit, row, columns[m] - pivot * row))
        columns = new
    return columns


def weighted_rows(weights, rows):
    total = weights[0] * rows[0]
    for weight, row in zip(weights[1:], rows[1:]):
        total = total + weight * row
    return total


def inverse_kernel(order_ref, top_ref, peer_ref, out_ref, a_ref):
    n = a_ref.shape[0]
    h = n // 2
    a_ref[:h, :] = top_ref[...]
    a_ref[h:, :h] = peer_ref[:, h:]
    a_ref[h:, h:] = peer_ref[:, :h]
    sub = lax.broadcasted_iota(jnp.int32, (SUB, 128), 0)
    lane = lax.broadcasted_iota(jnp.int32, (SUB, 128), 1)
    wide = lax.broadcasted_iota(jnp.int32, (1, 128), 1)
    for r in range(0, n, SUB):
        at = slice(r // 128 * 128, r // 128 * 128 + 128)
        a_ref[r : r + SUB, at] += jnp.where(lane == sub + r % 128, REG, 0.0)

    panels = BLOCK // SUB
    ahead = None
    for r0 in range(0, n, BLOCK):
        side = r0 // 128
        base = r0 % 128
        panel = []
        for q in range(panels):
            rows = slice(r0 + q * SUB, r0 + (q + 1) * SUB)
            panel.append([a_ref[rows, :128], a_ref[rows, 128:]])
        if ahead is not None:
            panel[0] = ahead
        for q in range(panels):
            k = base + q * SUB
            inside = (lane >= k) & (lane < k + SUB)
            small = small_inverse([spread(panel[q][side][:, k + m : k + m + 1]) for m in range(SUB)], sub)
            fresh = []
            for s in range(2):
                value = weighted_rows(small, [spread(panel[q][s][m : m + 1, :]) for m in range(SUB)])
                if s == side:
                    for m in range(SUB):
                        value = jnp.where(lane == k + m, small[m], value)
                fresh.append(value)
            panel[q] = fresh
            rows = [[spread(fresh[s][m : m + 1, :]) for m in range(SUB)] for s in range(2)]
            for i in range(panels):
                if i == q:
                    continue
                left = [spread(panel[i][side][:, k + m : k + m + 1]) for m in range(SUB)]
                for s in range(2):
                    old = panel[i][s]
                    if s == side:
                        old = jnp.where(inside, 0.0, old)
                    panel[i][s] = old - weighted_rows(left, rows[s])
        block = jnp.concatenate([jnp.concatenate(panel[q], axis=1) for q in range(panels)], axis=0)
        r1 = r0 + BLOCK
        inside = (wide >= base) & (wide < base + BLOCK)

        def update(low, high):
            change = jnp.dot(
                a_ref[low:high, r0:r1], block, preferred_element_type=jnp.float32, precision=lax.Precision.HIGHEST
            )
            for s in range(2):
                at = slice(s * 128, (s + 1) * 128)
                old = a_ref[low:high, at]
                if s == side:
                    old = jnp.where(inside, 0.0, old)
                a_ref[low:high, at] = old - change[:, at]

        if r1 < n:
            left = [spread(a_ref[r1 : r1 + SUB, r0 + m : r0 + m + 1]) for m in range(BLOCK)]
            ahead = []
            for s in range(2):
                old = a_ref[r1 : r1 + SUB, s * 128 : (s + 1) * 128]
                if s == side:
                    old = jnp.where((lane >= base) & (lane < base + BLOCK), 0.0, old)
                change = None
                for q in range(panels):
                    rows = [spread(panel[q][s][m : m + 1, :]) for m in range(SUB)]
                    part = weighted_rows(left[q * SUB : (q + 1) * SUB], rows)
                    change = part if change is None else change + part
                ahead.append(old - change)
            update(r1, r1 + BLOCK)
            if r1 + BLOCK < n:
                update(r1 + BLOCK, n)
        if r0 > 0:
            update(0, r0)
        a_ref[r0:r1, :] = block

    for b in range(n // 8):
        out_ref[pl.ds(pl.multiple_of(order_ref[b] * 8, 8), 8), :] = a_ref[b * 8 : (b + 1) * 8, :]


def ordered_inverse(order, top, peer):
    n = top.shape[1]
    return pl.pallas_call(
        inverse_kernel,
        out_shape=jax.ShapeDtypeStruct((n, n), jnp.float32),
        in_specs=[pl.BlockSpec(memory_space=pltpu.SMEM), whole(), whole()],
        out_specs=whole(),
        scratch_shapes=[pltpu.VMEM((n, n), jnp.float32)],
        compiler_params=pltpu.CompilerParams(vmem_limit_bytes=4 << 20),
        cost_estimate=pl.CostEstimate(flops=2 * 10**9, bytes_accessed=0, transcendentals=0),
        name="ordered_inverse",
    )(order, top, peer)


def final_kernel(rhs_ref, more_ref, inverse_ref, out_ref):
    out_ref[...] = lax.dot_general(
        rhs_ref[...] + more_ref[...],
        inverse_ref[...],
        (((0,), (1,)), ((), ())),
        preferred_element_type=jnp.float32,
        precision=lax.Precision.HIGHEST,
    )


def final_solve(*values):
    k, items = values[0].shape
    return pl.pallas_call(
        final_kernel,
        out_shape=jax.ShapeDtypeStruct((items, k), jnp.float32),
        in_specs=[whole()] * len(values),
        out_specs=whole(),
        compiler_params=pltpu.CompilerParams(vmem_limit_bytes=8 << 20),
        name="final_solve",
    )(*values)


def swap(value, stage):
    return lax.ppermute(value, ("band", "item"), band_perm(stage))


def body(ratings, rating_mask, attributes, attribute_mask, user_factors, tag_factors):
    n_users = user_factors.shape[0]
    own = jnp.concatenate([user_factors.T, tag_factors.T], axis=1)
    first, second = gather_columns(own)
    other_first = lax.ppermute(first, "item", CORE)
    other_second = lax.ppermute(second, "item", CORE)
    mine = jnp.concatenate([first, second], axis=0)
    other = jnp.concatenate([other_first, other_second], axis=0)

    parts = [
        masked(ratings, rating_mask, 1.0, "mask_users"),
        masked(attributes, attribute_mask, LAMBDA, "mask_tags"),
    ]

    item = lax.axis_index("item")
    y, z, c = item // (NZ * NC), (item // NC) % NZ, item % NC
    dc = jnp.repeat(jnp.arange(2, dtype=jnp.int32), 16)
    dy = jnp.array([p[0] for p in PLACES] * 2, jnp.int32)
    dz = jnp.array([p[1] + NZ for p in PLACES] * 2, jnp.int32)
    order = (((y + dy) % NY) * NZ + (z + dz) % NZ) * NC + (c + dc) % NC

    rhs_mine = rhs_rows(mine, parts, "rhs_mine")
    top = top_gram(own_gram(mine, n_users), mine, other, n_users)
    top, later = lax.optimization_barrier((top, other))
    rhs_other = rhs_rows(later, parts, "rhs_other")

    fresh, peer_mine, peer_other = lax.optimization_barrier((swap(top, 0), swap(rhs_mine, 0), swap(rhs_other, 0)))
    top = top + fresh
    rhs = jnp.concatenate([rhs_mine + peer_mine, rhs_other + peer_other], axis=0)
    top = top + swap(top, 2)
    rhs = rhs + swap(rhs, 1)
    top = top + swap(top, 1)
    inverse = ordered_inverse(order, top, lax.ppermute(top, "item", CORE))
    return final_solve(rhs, swap(rhs, 2), inverse)


def solution(mesh):
    spec = P("band", "item")
    return jax.shard_map(
        body, mesh=mesh, in_specs=(spec,) * 6, out_specs=P("item", None), check_vma=False
    )
```
